256 devices in a mesh: blk: 64 (over z, y, x_lo), hop: 4 (over x_hi, core).
Axes of the slice: x: 4 (x_hi: 2, x_lo: 2; x = x_hi * 2 + x_lo), y: 4, z: 8, core: 2. Of those that a mesh axis runs over, the one named last changes fastest.
Arguments:
- user_factors: float32 [196608, 256], P(('blk', 'hop')), may hold values from -1.5 to 1.5
- item_factors: float32 [131072, 256], P(('blk', 'hop')), may hold values from -1.5 to 1.5
- ratings: bfloat16 [196608, 5, 512], P(('blk', 'hop')), may hold values from -4 to 4, as said below
- block_mask: int32 [1536, 5, 4], P(('blk', 'hop')), may hold values from 0 to 1, as said below
Outputs:
- new_users: float32 [196608, 256], P(('blk', 'hop'))
- new_items: float32 [131072, 256], P(('blk', 'hop'))
The draws below stay inside these ranges and needn't reach their ends.
Inputs may be any that keep to these rules, and one draw needn't show every extreme that they name: `ratings`: zero marks a rating that is not observed; every other entry has magnitude 0.05 or more. `block_mask`: 1 marks a 128-square block that holds ratings; in every stratum some user shard has all of its blocks marked.
All inputs are finite; a program needn't handle non-finite values.
Results may differ from the reference program's by a relative error of at most 0.0024.
Values sent between devices are 32-bit elements; how exact they have to be, the bound alone decides.
A program may use at most 64 MiB of HBM per device.

```python
import jax
import jax.numpy as jnp
import numpy as np
from jax import lax

K = 256
BS = 128
IB = 512
ROWS_DEV = 768
STRATA = 5
USERS = 196608
ITEMS = 131072
N_BLK = 64
N_HOP = 4


def factor_draw(key, shape):
    values = 0.25 * jax.random.normal(key, shape, jnp.float32)
    return jnp.clip(values, -1.5, 1.5)


def draw_user_factors(key, part):
    return factor_draw(jax.random.fold_in(key, 31), (USERS, K))


def draw_item_factors(key, part):
    return factor_draw(jax.random.fold_in(key, 32), (ITEMS, K))


def draw_ratings(key, part):
    shape = (USERS, STRATA, IB)
    key_values = jax.random.fold_in(key, 11)
    key_seen = jax.random.fold_in(key, 12)
    values = jax.random.normal(key_values, shape, jnp.float32)
    values = jnp.clip(values, -4.0, 4.0)
    values = jnp.where(jnp.abs(values) < 0.05, jnp.where(values < 0.0, -0.05, 0.05), values)
    seen = jax.random.randint(key_seen, shape, 0, 2)
    return jnp.where(seen == 1, values, 0.0).astype(jnp.bfloat16)


def draw_block_mask(key, part):
    shards = USERS // ROWS_DEV
    per_shard = ROWS_DEV // BS
    key_level = jax.random.fold_in(key, 21)
    key_full = jax.random.fold_in(key, 22)
    key_coin = jax.random.fold_in(key, 23)
    levels = jax.random.randint(key_level, (shards,), 2, 5)
    fullest = jax.random.randint(key_full, (), 0, shards)
    levels = jnp.where(jnp.arange(shards) == fullest, 4, levels)
    level_rows = jnp.repeat(levels, per_shard, total_repeat_length=shards * per_shard)
    coins = jax.random.randint(key_coin, (USERS // BS, STRATA, IB // BS), 0, 4)
    return (coins < level_rows[:, None, None]).astype(jnp.int32)


def setup_inputs(seed: int = 0) -> dict:
    arg_keys = jax.random.split(jax.random.key(seed), 5)
    user_factors = draw_user_factors(jax.random.fold_in(arg_keys[4], 71), 0)
    item_factors = draw_item_factors(jax.random.fold_in(arg_keys[4], 71), 0)
    ratings = draw_ratings(jax.random.fold_in(arg_keys[4], 71), 0)
    block_mask = draw_block_mask(jax.random.fold_in(arg_keys[4], 71), 0)
    return {"user_factors": user_factors, "item_factors": item_factors, "ratings": ratings, "block_mask": block_mask}


CLIP_LIMIT = 3.0
DECAY = 0.03
RATE = 4.0


def errors(user_bf, item_bf, tile_rates, observed):
    predicted = jnp.dot(user_bf, item_bf.T, preferred_element_type=jnp.float32)
    misfit = jnp.clip(tile_rates.astype(jnp.float32) - predicted, -CLIP_LIMIT, CLIP_LIMIT)
    return jnp.where(observed, misfit, 0.0).astype(jnp.bfloat16)


def expand(tile_rates, tile_flags):
    row_blocks, col_blocks = tile_flags.shape
    nonzero = tile_rates.reshape(row_blocks, BS, col_blocks, BS) != 0
    return (nonzero & (tile_flags[:, None, :, None] > 0)).reshape(tile_rates.shape)


def update_tile(operands):
    user_rows, item_rows, tile_rates, tile_flags = operands
    observed = expand(tile_rates, tile_flags)
    user_bf = user_rows.astype(jnp.bfloat16)
    item_bf = item_rows.astype(jnp.bfloat16)
    misfit = errors(user_bf, item_bf, tile_rates, observed)
    gradient = jnp.dot(misfit, item_bf, preferred_element_type=jnp.float32)
    user_rows = (1.0 - DECAY) * user_rows + (RATE / IB) * gradient
    user_bf = user_rows.astype(jnp.bfloat16)
    misfit = errors(user_bf, item_bf, tile_rates, observed)
    gradient = jnp.dot(misfit.T, user_bf, preferred_element_type=jnp.float32)
    item_rows = (1.0 - DECAY) * item_rows + (RATE / ROWS_DEV) * gradient
    return user_rows, item_rows


def reference(user_factors, item_factors, ratings, block_mask):
    devices = N_BLK * N_HOP
    user_rows = user_factors.reshape(devices, ROWS_DEV, K)
    item_rows = item_factors.reshape(devices, IB, K)
    rates_all = ratings.reshape(devices, ROWS_DEV, STRATA, IB)
    flags_all = block_mask.reshape(devices, ROWS_DEV // BS, STRATA, IB // BS)
    device_ids = np.arange(devices)
    blk_index = device_ids // N_HOP
    hop_index = device_ids % N_HOP
    for stratum in range(STRATA):
        blk_back = min(stratum, STRATA - 2)
        hop_back = 1 if stratum == STRATA - 1 else 0
        source = ((blk_index - blk_back) % N_BLK) * N_HOP + (hop_index - hop_back) % N_HOP
        inverse = np.argsort(source)
        visiting = item_rows[source]
        user_rows, visiting = lax.map(update_tile, (user_rows, visiting, rates_all[:, :, stratum, :], flags_all[:, :, stratum, :]))
        item_rows = visiting[inverse]
    return user_rows.reshape(USERS, K), item_rows.reshape(ITEMS, K)
```

```python
import jax
import jax.numpy as jnp
from jax import lax
from jax.sharding import PartitionSpec as P

CLIP_LIMIT = 3.0
DECAY = 0.03
RATE = 4.0
CHUNK = 128


def shift(block, axes, sizes, offsets):
    total = 1
    for size in sizes:
        total *= size
    route = []
    for src in range(total):
        coords = []
        rem = src
        for size in reversed(sizes):
            coords.append(rem % size)
            rem //= size
        coords = coords[::-1]
        dst = 0
        for c, size, off in zip(coords, sizes, offsets):
            dst = dst * size + (c + off) % size
        route.append((src, dst))
    return lax.ppermute(block, axes, route)


def errors(user_bf, item_bf, tile_rates, observed):
    predicted = jnp.einsum("ik,jk->ij", user_bf, item_bf, preferred_element_type=jnp.float32)
    misfit = jnp.clip(tile_rates.astype(jnp.float32) - predicted, -CLIP_LIMIT, CLIP_LIMIT)
    return jnp.where(observed, misfit, 0.0).astype(jnp.bfloat16)


def expand(tile_rates, tile_flags):
    row_blocks, col_blocks = tile_flags.shape
    block_side = tile_rates.shape[0] // row_blocks
    col_side = tile_rates.shape[1] // col_blocks
    nonzero = tile_rates.reshape(row_blocks, block_side, col_blocks, col_side) != 0
    return (nonzero & (tile_flags[:, None, :, None] > 0)).reshape(tile_rates.shape)


def body(user_factors, item_factors, ratings, block_mask):
    row_count = user_factors.shape[0]
    item_count = item_factors.shape[0]
    strata = ratings.shape[1]
    user_rate = RATE / item_count
    item_rate = RATE / row_count
    n_blk = lax.axis_size("blk")
    n_hop = lax.axis_size("hop")
    n_chunks = item_count // CHUNK
    flag_cols = block_mask.shape[2] // n_chunks
    user_rows = user_factors
    chunks = [item_factors[k * CHUNK:(k + 1) * CHUNK] for k in range(n_chunks)]
    for stratum in range(strata):
        tile_rates = ratings[:, stratum, :]
        tile_flags = block_mask[:, stratum, :]
        rates_k = [tile_rates[:, k * CHUNK:(k + 1) * CHUNK] for k in range(n_chunks)]
        observed_k = [
            expand(rates_k[k], tile_flags[:, k * flag_cols:(k + 1) * flag_cols]) for k in range(n_chunks)
        ]
        items_bf = [c.astype(jnp.bfloat16) for c in chunks]
        user_bf = user_rows.astype(jnp.bfloat16)
        gradient = None
        for k in range(n_chunks):
            misfit = errors(user_bf, items_bf[k], rates_k[k], observed_k[k])
            part = jnp.dot(misfit, items_bf[k], preferred_element_type=jnp.float32)
            gradient = part if gradient is None else gradient + part
        user_rows = (1.0 - DECAY) * user_rows + user_rate * gradient
        user_bf = user_rows.astype(jnp.bfloat16)
        updated = []
        for k in range(n_chunks):
            misfit = errors(user_bf, items_bf[k], rates_k[k], observed_k[k])
            grad_k = jnp.einsum("ij,ik->jk", misfit, user_bf, preferred_element_type=jnp.float32)
            new_k = (1.0 - DECAY) * chunks[k] + item_rate * grad_k
            if stratum < strata - 2:
                new_k = shift(new_k, "blk", (n_blk,), (1,))
            elif stratum == strata - 2:
                new_k = shift(new_k, "hop", (n_hop,), (1,))
            updated.append(new_k)
        chunks = updated
    back = strata - 2
    returned = [shift(c, ("blk", "hop"), (n_blk, n_hop), (-back, -1)) for c in chunks]
    return (user_rows, jnp.concatenate(returned, axis=0))


def solution(mesh):
    in_specs = (
        P(("blk", "hop"), None),
        P(("blk", "hop"), None),
        P(("blk", "hop"), None, None),
        P(("blk", "hop"), None, None),
    )
    out_specs = (P(("blk", "hop"), None), P(("blk", "hop"), None))
    return jax.shard_map(body, mesh=mesh, in_specs=in_specs, out_specs=out_specs, check_vma=False)
```

```python
import functools

import jax
import jax.numpy as jnp
from jax import lax
from jax.experimental import pallas as pl
from jax.experimental.pallas import tpu as pltpu
from jax.sharding import PartitionSpec as P

CLIP_LIMIT = 3.0
DECAY = 0.03
RATE = 4.0


def shift(block, axes, sizes, offsets):
    total = 1
    for size in sizes:
        total *= size
    route = []
    for src in range(total):
        coords = []
        rem = src
        for size in reversed(sizes):
            coords.append(rem % size)
            rem //= size
        coords = coords[::-1]
        dst = 0
        for c, size, off in zip(coords, sizes, offsets):
            dst = dst * size + (c + off) % size
        route.append((src, dst))
    return lax.ppermute(block, axes, route)


def tile_kernel(user_rate, item_rate, flags_ref, users_ref, items_ref, rates_ref, users_out, items_out, obs_ref):
    row_blocks, col_blocks = flags_ref.shape
    rows, cols = rates_ref.shape
    bs_r = rows // row_blocks
    bs_c = cols // col_blocks
    for r in range(row_blocks):
        for c in range(col_blocks):
            block = rates_ref[r * bs_r:(r + 1) * bs_r, c * bs_c:(c + 1) * bs_c]
            keep = jnp.logical_and(block != 0, flags_ref[r, c] > 0)
            obs_ref[r * bs_r:(r + 1) * bs_r, c * bs_c:(c + 1) * bs_c] = keep.astype(jnp.float32)
    observed = obs_ref[...] > 0
    rates = rates_ref[...].astype(jnp.float32)
    user_rows = users_ref[...]
    item_rows = items_ref[...]
    item_bf = item_rows.astype(jnp.bfloat16)
    user_bf = user_rows.astype(jnp.bfloat16)
    nt = (((1,), (1,)), ((), ()))
    predicted = lax.dot_general(user_bf, item_bf, nt, preferred_element_type=jnp.float32)
    misfit = jnp.where(observed, jnp.clip(rates - predicted, -CLIP_LIMIT, CLIP_LIMIT), 0.0).astype(jnp.bfloat16)
    gradient = jnp.dot(misfit, item_bf, preferred_element_type=jnp.float32)
    user_rows = (1.0 - DECAY) * user_rows + user_rate * gradient
    users_out[...] = user_rows
    user_bf = user_rows.astype(jnp.bfloat16)
    predicted = lax.dot_general(user_bf, item_bf, nt, preferred_element_type=jnp.float32)
    misfit = jnp.where(observed, jnp.clip(rates - predicted, -CLIP_LIMIT, CLIP_LIMIT), 0.0).astype(jnp.bfloat16)
    tn = (((0,), (0,)), ((), ()))
    gradient = lax.dot_general(misfit, user_bf, tn, preferred_element_type=jnp.float32)
    items_out[...] = (1.0 - DECAY) * item_rows + item_rate * gradient


def update_tile(user_rows, item_rows, tile_rates, tile_flags, user_rate, item_rate):
    rows, k = user_rows.shape
    cols = item_rows.shape[0]
    flops = 8 * rows * cols * k
    nbytes = 2 * (rows * k * 4 + cols * k * 4) + rows * cols * 2
    vmem = pl.BlockSpec(memory_space=pltpu.VMEM)
    return pl.pallas_call(
        functools.partial(tile_kernel, user_rate, item_rate),
        out_shape=(
            jax.ShapeDtypeStruct(user_rows.shape, jnp.float32),
            jax.ShapeDtypeStruct(item_rows.shape, jnp.float32),
        ),
        in_specs=[pl.BlockSpec(memory_space=pltpu.SMEM), vmem, vmem, vmem],
        out_specs=(vmem, vmem),
        scratch_shapes=[pltpu.VMEM((rows, cols), jnp.float32)],
        cost_estimate=pl.CostEstimate(flops=flops, bytes_accessed=nbytes, transcendentals=0),
    )(tile_flags, user_rows, item_rows, tile_rates)


def body(user_factors, item_factors, ratings, block_mask):
    row_count = user_factors.shape[0]
    item_count = item_factors.shape[0]
    strata = ratings.shape[1]
    user_rate = RATE / item_count
    item_rate = RATE / row_count
    n_blk = lax.axis_size("blk")
    n_hop = lax.axis_size("hop")
    user_rows = user_factors
    item_rows = item_factors
    for stratum in range(strata):
        tile_rates = ratings[:, stratum, :]
        tile_flags = block_mask[:, stratum, :]
        user_rows, item_rows = update_tile(user_rows, item_rows, tile_rates, tile_flags, user_rate, item_rate)
        if stratum < strata - 2:
            item_rows = shift(item_rows, "blk", (n_blk,), (1,))
        elif stratum == strata - 2:
            item_rows = shift(item_rows, "hop", (n_hop,), (1,))
    back = strata - 2
    returned = shift(item_rows, ("blk", "hop"), (n_blk, n_hop), (-back, -1))
    return (user_rows, returned)


def solution(mesh):
    in_specs = (
        P(("blk", "hop"), None),
        P(("blk", "hop"), None),
        P(("blk", "hop"), None, None),
        P(("blk", "hop"), None, None),
    )
    out_specs = (P(("blk", "hop"), None), P(("blk", "hop"), None))
    return jax.shard_map(body, mesh=mesh, in_specs=in_specs, out_specs=out_specs, check_vma=False)
```

```python
import functools

import jax
import jax.numpy as jnp
from jax import lax
from jax.experimental import pallas as pl
from jax.experimental.pallas import tpu as pltpu
from jax.sharding import PartitionSpec as P

CLIP_LIMIT = 3.0
DECAY = 0.03
RATE = 4.0


def shift(block, axes, sizes, offsets):
    total = 1
    for size in sizes:
        total *= size
    route = []
    for src in range(total):
        coords = []
        rem = src
        for size in reversed(sizes):
            coords.append(rem % size)
            rem //= size
        coords = coords[::-1]
        dst = 0
        for c, size, off in zip(coords, sizes, offsets):
            dst = dst * size + (c + off) % size
        route.append((src, dst))
    return lax.ppermute(block, axes, route)


def tile_kernel(user_rate, item_rate, flags_ref, users_ref, items_ref, rates_ref, users_out, items_out, obs_ref):
    row_blocks, col_blocks = flags_ref.shape
    rows, cols = rates_ref.shape
    bs_r = rows // row_blocks
    bs_c = cols // col_blocks
    for r in range(row_blocks):
        for c in range(col_blocks):
            block = rates_ref[r * bs_r:(r + 1) * bs_r, c * bs_c:(c + 1) * bs_c]
            keep = jnp.logical_and(block != 0, flags_ref[r, c] > 0)
            obs_ref[r * bs_r:(r + 1) * bs_r, c * bs_c:(c + 1) * bs_c] = keep.astype(jnp.float32)
    observed = obs_ref[...] > 0
    rates = rates_ref[...].astype(jnp.float32)
    user_rows = users_ref[...]
    item_rows = items_ref[...]
    item_bf = item_rows.astype(jnp.bfloat16)
    user_bf = user_rows.astype(jnp.bfloat16)
    nt = (((1,), (1,)), ((), ()))
    predicted = lax.dot_general(user_bf, item_bf, nt, preferred_element_type=jnp.float32)
    misfit = jnp.where(observed, jnp.clip(rates - predicted, -CLIP_LIMIT, CLIP_LIMIT), 0.0).astype(jnp.bfloat16)
    gradient = jnp.dot(misfit, item_bf, preferred_element_type=jnp.float32)
    user_rows = (1.0 - DECAY) * user_rows + user_rate * gradient
    users_out[...] = user_rows
    user_bf = user_rows.astype(jnp.bfloat16)
    predicted = lax.dot_general(user_bf, item_bf, nt, preferred_element_type=jnp.float32)
    misfit = jnp.where(observed, jnp.clip(rates - predicted, -CLIP_LIMIT, CLIP_LIMIT), 0.0).astype(jnp.bfloat16)
    tn = (((0,), (0,)), ((), ()))
    gradient = lax.dot_general(misfit, user_bf, tn, preferred_element_type=jnp.float32)
    items_out[...] = (1.0 - DECAY) * item_rows + item_rate * gradient


def update_tile(user_rows, item_rows, tile_rates, tile_flags, user_rate, item_rate):
    rows, k = user_rows.shape
    cols = item_rows.shape[0]
    flops = 8 * rows * cols * k
    nbytes = 2 * (rows * k * 4 + cols * k * 4) + rows * cols * 2
    vmem = pl.BlockSpec(memory_space=pltpu.VMEM)
    return pl.pallas_call(
        functools.partial(tile_kernel, user_rate, item_rate),
        out_shape=(
            jax.ShapeDtypeStruct(user_rows.shape, jnp.float32),
            jax.ShapeDtypeStruct(item_rows.shape, jnp.float32),
        ),
        in_specs=[pl.BlockSpec(memory_space=pltpu.SMEM), vmem, vmem, vmem],
        out_specs=(vmem, vmem),
        scratch_shapes=[pltpu.VMEM((rows, cols), jnp.float32)],
        cost_estimate=pl.CostEstimate(flops=flops, bytes_accessed=nbytes, transcendentals=0),
    )(tile_flags, user_rows, item_rows, tile_rates)


def body(user_factors, item_factors, ratings, block_mask):
    row_count = user_factors.shape[0]
    item_count = item_factors.shape[0]
    strata = ratings.shape[1]
    user_rate = RATE / item_count
    item_rate = RATE / row_count
    n_blk = lax.axis_size("blk")
    n_hop = lax.axis_size("hop")
    user_rows = user_factors
    item_rows = item_factors
    for stratum in range(strata):
        rates_src, flags_src = ratings, block_mask
        if stratum > 0:
            rates_src, flags_src, user_rows = lax.optimization_barrier((ratings, block_mask, user_rows))
        tile_rates = rates_src[:, stratum, :]
        tile_flags = flags_src[:, stratum, :]
        user_rows, item_rows = update_tile(user_rows, item_rows, tile_rates, tile_flags, user_rate, item_rate)
        if stratum < strata - 2:
            item_rows = shift(item_rows, "blk", (n_blk,), (1,))
        elif stratum == strata - 2:
            item_rows = shift(item_rows, "hop", (n_hop,), (1,))
    back = strata - 2
    returned = shift(item_rows, ("blk", "hop"), (n_blk, n_hop), (-back, -1))
    return (user_rows, returned)


def solution(mesh):
    in_specs = (
        P(("blk", "hop"), None),
        P(("blk", "hop"), None),
        P(("blk", "hop"), None, None),
        P(("blk", "hop"), None, None),
    )
    out_specs = (P(("blk", "hop"), None), P(("blk", "hop"), None))
    return jax.shard_map(body, mesh=mesh, in_specs=in_specs, out_specs=out_specs, check_vma=False)
```

```python
import functools

import jax
import jax.numpy as jnp
from jax import lax
from jax.experimental import pallas as pl
from jax.experimental.pallas import tpu as pltpu
from jax.sharding import PartitionSpec as P

CLIP_LIMIT = 3.0
DECAY = 0.03
RATE = 4.0


def shift(block, axes, sizes, offsets):
    total = 1
    for size in sizes:
        total *= size
    route = []
    for src in range(total):
        coords = []
        rem = src
        for size in reversed(sizes):
            coords.append(rem % size)
            rem //= size
        coords = coords[::-1]
        dst = 0
        for c, size, off in zip(coords, sizes, offsets):
            dst = dst * size + (c + off) % size
        route.append((src, dst))
    return lax.ppermute(block, axes, route)


def tile_kernel(user_rate, item_rate, flags_ref, users_ref, items_ref, rates_ref, users_out, items_out):
    row_blocks, col_blocks = flags_ref.shape
    rows, cols = rates_ref.shape
    bs_r = rows // row_blocks
    bs_c = cols // col_blocks
    item_rows = items_ref[...]
    item_bf = item_rows.astype(jnp.bfloat16)
    nt = (((1,), (1,)), ((), ()))
    tn = (((0,), (0,)), ((), ()))
    column_block = lax.broadcasted_iota(jnp.int32, (1, cols), 1) // bs_c
    total = None
    for r in range(row_blocks):
        lo, hi = r * bs_r, (r + 1) * bs_r
        col_flag = jnp.zeros((1, cols), jnp.int32)
        for c in range(col_blocks):
            col_flag = jnp.where(column_block == c, flags_ref[r, c], col_flag)
        block = rates_ref[lo:hi, :]
        observed = jnp.logical_and(block != 0, col_flag > 0)
        rates = block.astype(jnp.float32)
        user_rows = users_ref[lo:hi, :]
        user_bf = user_rows.astype(jnp.bfloat16)
        predicted = lax.dot_general(user_bf, item_bf, nt, preferred_element_type=jnp.float32)
        misfit = jnp.where(observed, jnp.clip(rates - predicted, -CLIP_LIMIT, CLIP_LIMIT), 0.0)
        gradient = jnp.dot(misfit.astype(jnp.bfloat16), item_bf, preferred_element_type=jnp.float32)
        user_rows = (1.0 - DECAY) * user_rows + user_rate * gradient
        users_out[lo:hi, :] = user_rows
        user_bf = user_rows.astype(jnp.bfloat16)
        predicted = lax.dot_general(user_bf, item_bf, nt, preferred_element_type=jnp.float32)
        misfit = jnp.where(observed, jnp.clip(rates - predicted, -CLIP_LIMIT, CLIP_LIMIT), 0.0)
        part = lax.dot_general(misfit.astype(jnp.bfloat16), user_bf, tn, preferred_element_type=jnp.float32)
        total = part if total is None else total + part
    items_out[...] = (1.0 - DECAY) * item_rows + item_rate * total


def update_tile(user_rows, item_rows, tile_rates, tile_flags, user_rate, item_rate):
    rows, k = user_rows.shape
    cols = item_rows.shape[0]
    flops = 8 * rows * cols * k
    nbytes = 2 * (rows * k * 4 + cols * k * 4) + rows * cols * 2
    vmem = pl.BlockSpec(memory_space=pltpu.VMEM)
    return pl.pallas_call(
        functools.partial(tile_kernel, user_rate, item_rate),
        out_shape=(
            jax.ShapeDtypeStruct(user_rows.shape, jnp.float32),
            jax.ShapeDtypeStruct(item_rows.shape, jnp.float32),
        ),
        in_specs=[pl.BlockSpec(memory_space=pltpu.SMEM), vmem, vmem, vmem],
        out_specs=(vmem, vmem),
        cost_estimate=pl.CostEstimate(flops=flops, bytes_accessed=nbytes, transcendentals=0),
    )(tile_flags, user_rows, item_rows, tile_rates)


def body(user_factors, item_factors, ratings, block_mask):
    row_count = user_factors.shape[0]
    item_count = item_factors.shape[0]
    strata = ratings.shape[1]
    user_rate = RATE / item_count
    item_rate = RATE / row_count
    n_blk = lax.axis_size("blk")
    n_hop = lax.axis_size("hop")
    user_rows = user_factors
    item_rows = item_factors
    for stratum in range(strata):
        rates_src, flags_src = ratings, block_mask
        if stratum > 0:
            rates_src, flags_src, user_rows = lax.optimization_barrier((ratings, block_mask, user_rows))
        tile_rates = rates_src[:, stratum, :]
        tile_flags = flags_src[:, stratum, :]
        user_rows, item_rows = update_tile(user_rows, item_rows, tile_rates, tile_flags, user_rate, item_rate)
        if stratum < strata - 2:
            item_rows = shift(item_rows, "blk", (n_blk,), (1,))
        elif stratum == strata - 2:
            item_rows = shift(item_rows, "hop", (n_hop,), (1,))
    back = strata - 2
    returned = shift(item_rows, ("blk", "hop"), (n_blk, n_hop), (-back, -1))
    return (user_rows, returned)


def solution(mesh):
    in_specs = (
        P(("blk", "hop"), None),
        P(("blk", "hop"), None),
        P(("blk", "hop"), None, None),
        P(("blk", "hop"), None, None),
    )
    out_specs = (P(("blk", "hop"), None), P(("blk", "hop"), None))
    return jax.shard_map(body, mesh=mesh, in_specs=in_specs, out_specs=out_specs, check_vma=False)
```

```python
import functools

import jax
import jax.numpy as jnp
from jax import lax
from jax.experimental import pallas as pl
from jax.experimental.pallas import tpu as pltpu
from jax.sharding import PartitionSpec as P

CLIP_LIMIT = 3.0
DECAY = 0.03
RATE = 4.0


def shift(block, axes, sizes, offsets):
    total = 1
    for size in sizes:
        total *= size
    route = []
    for src in range(total):
        coords = []
        rem = src
        for size in reversed(sizes):
            coords.append(rem % size)
            rem //= size
        coords = coords[::-1]
        dst = 0
        for c, size, off in zip(coords, sizes, offsets):
            dst = dst * size + (c + off) % size
        route.append((src, dst))
    return lax.ppermute(block, axes, route)


def tile_kernel(user_rate, item_rate, users_ref, items_ref, rates_ref, seen_ref, users_out, items_out):
    rates = rates_ref[...]
    seen = seen_ref[...]
    user_rows = users_ref[...]
    item_rows = items_ref[...]
    item_bf = item_rows.astype(jnp.bfloat16)
    user_bf = user_rows.astype(jnp.bfloat16)
    nt = (((1,), (1,)), ((), ()))
    predicted = lax.dot_general(user_bf, item_bf, nt, preferred_element_type=jnp.float32)
    misfit = (jnp.clip(rates - predicted, -CLIP_LIMIT, CLIP_LIMIT) * seen).astype(jnp.bfloat16)
    gradient = jnp.dot(misfit, item_bf, preferred_element_type=jnp.float32)
    user_rows = (1.0 - DECAY) * user_rows + user_rate * gradient
    users_out[...] = user_rows
    user_bf = user_rows.astype(jnp.bfloat16)
    predicted = lax.dot_general(user_bf, item_bf, nt, preferred_element_type=jnp.float32)
    misfit = (jnp.clip(rates - predicted, -CLIP_LIMIT, CLIP_LIMIT) * seen).astype(jnp.bfloat16)
    tn = (((0,), (0,)), ((), ()))
    gradient = lax.dot_general(misfit, user_bf, tn, preferred_element_type=jnp.float32)
    items_out[...] = (1.0 - DECAY) * item_rows + item_rate * gradient


def expand(tile_rates, tile_flags):
    row_blocks, col_blocks = tile_flags.shape
    block_rows = tile_rates.shape[0] // row_blocks
    block_cols = tile_rates.shape[1] // col_blocks
    nonzero = tile_rates.reshape(row_blocks, block_rows, col_blocks, block_cols) != 0
    return (nonzero & (tile_flags[:, None, :, None] > 0)).reshape(tile_rates.shape)


def update_tile(user_rows, item_rows, tile_rates, tile_flags, user_rate, item_rate):
    rows, k = user_rows.shape
    cols = item_rows.shape[0]
    seen = expand(tile_rates, tile_flags).astype(jnp.float32)
    rates = tile_rates.astype(jnp.float32)
    flops = 8 * rows * cols * k
    nbytes = 2 * (rows * k * 4 + cols * k * 4) + 2 * rows * cols * 4
    vmem = pl.BlockSpec(memory_space=pltpu.VMEM)
    return pl.pallas_call(
        functools.partial(tile_kernel, user_rate, item_rate),
        out_shape=(
            jax.ShapeDtypeStruct(user_rows.shape, jnp.float32),
            jax.ShapeDtypeStruct(item_rows.shape, jnp.float32),
        ),
        in_specs=[vmem, vmem, vmem, vmem],
        out_specs=(vmem, vmem),
        cost_estimate=pl.CostEstimate(flops=flops, bytes_accessed=nbytes, transcendentals=0),
    )(user_rows, item_rows, rates, seen)


def body(user_factors, item_factors, ratings, block_mask):
    row_count = user_factors.shape[0]
    item_count = item_factors.shape[0]
    strata = ratings.shape[1]
    user_rate = RATE / item_count
    item_rate = RATE / row_count
    n_blk = lax.axis_size("blk")
    n_hop = lax.axis_size("hop")
    user_rows = user_factors
    item_rows = item_factors
    for stratum in range(strata):
        rates_src, flags_src = ratings, block_mask
        if stratum > 0:
            rates_src, user_rows = lax.optimization_barrier((ratings, user_rows))
        tile_rates = rates_src[:, stratum, :]
        tile_flags = flags_src[:, stratum, :]
        user_rows, item_rows = update_tile(user_rows, item_rows, tile_rates, tile_flags, user_rate, item_rate)
        if stratum < strata - 2:
            item_rows = shift(item_rows, "blk", (n_blk,), (1,))
        elif stratum == strata - 2:
            item_rows = shift(item_rows, "hop", (n_hop,), (1,))
    back = strata - 2
    returned = shift(item_rows, ("blk", "hop"), (n_blk, n_hop), (-back, -1))
    return (user_rows, returned)


def solution(mesh):
    in_specs = (
        P(("blk", "hop"), None),
        P(("blk", "hop"), None),
        P(("blk", "hop"), None, None),
        P(("blk", "hop"), None, None),
    )
    out_specs = (P(("blk", "hop"), None), P(("blk", "hop"), None))
    return jax.shard_map(body, mesh=mesh, in_specs=in_specs, out_specs=out_specs, check_vma=False)
```

```python
import functools

import jax
import jax.numpy as jnp
from jax import lax
from jax.experimental import pallas as pl
from jax.experimental.pallas import tpu as pltpu
from jax.sharding import PartitionSpec as P

CLIP_LIMIT = 3.0
DECAY = 0.03
RATE = 4.0


def shift(block, axes, sizes, offsets):
    total = 1
    for size in sizes:
        total *= size
    route = []
    for src in range(total):
        coords = []
        rem = src
        for size in reversed(sizes):
            coords.append(rem % size)
            rem //= size
        coords = coords[::-1]
        dst = 0
        for c, size, off in zip(coords, sizes, offsets):
            dst = dst * size + (c + off) % size
        route.append((src, dst))
    return lax.ppermute(block, axes, route)


def tile_kernel(user_rate, item_rate, users_ref, items_ref, rates_ref, users_out, items_out):
    rates = rates_ref[...].astype(jnp.float32)
    observed = rates != 0
    user_rows = users_ref[...]
    item_rows = items_ref[...]
    item_bf = item_rows.astype(jnp.bfloat16)
    user_bf = user_rows.astype(jnp.bfloat16)
    nt = (((1,), (1,)), ((), ()))
    predicted = lax.dot_general(user_bf, item_bf, nt, preferred_element_type=jnp.float32)
    misfit = jnp.where(observed, jnp.clip(rates - predicted, -CLIP_LIMIT, CLIP_LIMIT), 0.0).astype(jnp.bfloat16)
    gradient = jnp.dot(misfit, item_bf, preferred_element_type=jnp.float32)
    user_rows = (1.0 - DECAY) * user_rows + user_rate * gradient
    users_out[...] = user_rows
    user_bf = user_rows.astype(jnp.bfloat16)
    predicted = lax.dot_general(user_bf, item_bf, nt, preferred_element_type=jnp.float32)
    misfit = jnp.where(observed, jnp.clip(rates - predicted, -CLIP_LIMIT, CLIP_LIMIT), 0.0).astype(jnp.bfloat16)
    tn = (((0,), (0,)), ((), ()))
    gradient = lax.dot_general(misfit, user_bf, tn, preferred_element_type=jnp.float32)
    items_out[...] = (1.0 - DECAY) * item_rows + item_rate * gradient


def mask_blocks(tile_rates, tile_flags):
    row_blocks, col_blocks = tile_flags.shape
    block_rows = tile_rates.shape[0] // row_blocks
    block_cols = tile_rates.shape[1] // col_blocks
    blocks = tile_rates.reshape(row_blocks, block_rows, col_blocks, block_cols)
    kept = jnp.where(tile_flags[:, None, :, None] > 0, blocks, jnp.zeros_like(blocks))
    return kept.reshape(tile_rates.shape)


def update_tile(user_rows, item_rows, tile_rates, tile_flags, user_rate, item_rate):
    rows, k = user_rows.shape
    cols = item_rows.shape[0]
    rates = mask_blocks(tile_rates, tile_flags)
    flops = 8 * rows * cols * k
    nbytes = 2 * (rows * k * 4 + cols * k * 4) + rows * cols * 2
    vmem = pl.BlockSpec(memory_space=pltpu.VMEM)
    return pl.pallas_call(
        functools.partial(tile_kernel, user_rate, item_rate),
        out_shape=(
            jax.ShapeDtypeStruct(user_rows.shape, jnp.float32),
            jax.ShapeDtypeStruct(item_rows.shape, jnp.float32),
        ),
        in_specs=[vmem, vmem, vmem],
        out_specs=(vmem, vmem),
        cost_estimate=pl.CostEstimate(flops=flops, bytes_accessed=nbytes, transcendentals=0),
    )(user_rows, item_rows, rates)


def body(user_factors, item_factors, ratings, block_mask):
    row_count = user_factors.shape[0]
    item_count = item_factors.shape[0]
    strata = ratings.shape[1]
    user_rate = RATE / item_count
    item_rate = RATE / row_count
    n_blk = lax.axis_size("blk")
    n_hop = lax.axis_size("hop")
    user_rows = user_factors
    item_rows = item_factors
    for stratum in range(strata):
        rates_src, flags_src = ratings, block_mask
        if stratum > 0:
            rates_src, user_rows = lax.optimization_barrier((ratings, user_rows))
        tile_rates = rates_src[:, stratum, :]
        tile_flags = flags_src[:, stratum, :]
        user_rows, item_rows = update_tile(user_rows, item_rows, tile_rates, tile_flags, user_rate, item_rate)
        if stratum < strata - 2:
            item_rows = shift(item_rows, "blk", (n_blk,), (1,))
        elif stratum == strata - 2:
            item_rows = shift(item_rows, "hop", (n_hop,), (1,))
    back = strata - 2
    returned = shift(item_rows, ("blk", "hop"), (n_blk, n_hop), (-back, -1))
    return (user_rows, returned)


def solution(mesh):
    in_specs = (
        P(("blk", "hop"), None),
        P(("blk", "hop"), None),
        P(("blk", "hop"), None, None),
        P(("blk", "hop"), None, None),
    )
    out_specs = (P(("blk", "hop"), None), P(("blk", "hop"), None))
    return jax.shard_map(body, mesh=mesh, in_specs=in_specs, out_specs=out_specs, check_vma=False)
```

```python
import functools

import jax
import jax.numpy as jnp
from jax import lax
from jax.experimental import pallas as pl
from jax.experimental.pallas import tpu as pltpu
from jax.sharding import PartitionSpec as P

CLIP_LIMIT = 3.0
DECAY = 0.03
RATE = 4.0


def shift(block, axes, sizes, offsets):
    total = 1
    for size in sizes:
        total *= size
    route = []
    for src in range(total):
        coords = []
        rem = src
        for size in reversed(sizes):
            coords.append(rem % size)
            rem //= size
        coords = coords[::-1]
        dst = 0
        for c, size, off in zip(coords, sizes, offsets):
            dst = dst * size + (c + off) % size
        route.append((src, dst))
    return lax.ppermute(block, axes, route)


def tile_kernel(user_rate, item_rate, users_ref, items_hbm, rates_ref, users_out, items_out, items_ref, sem):
    fetch = pltpu.make_async_copy(items_hbm, items_ref, sem)
    fetch.start()
    rates = rates_ref[...].astype(jnp.float32)
    observed = rates != 0
    user_rows = users_ref[...]
    fetch.wait()
    item_rows = items_ref[...]
    item_bf = item_rows.astype(jnp.bfloat16)
    user_bf = user_rows.astype(jnp.bfloat16)
    nt = (((1,), (1,)), ((), ()))
    predicted = lax.dot_general(user_bf, item_bf, nt, preferred_element_type=jnp.float32)
    misfit = jnp.where(observed, jnp.clip(rates - predicted, -CLIP_LIMIT, CLIP_LIMIT), 0.0).astype(jnp.bfloat16)
    gradient = jnp.dot(misfit, item_bf, preferred_element_type=jnp.float32)
    user_rows = (1.0 - DECAY) * user_rows + user_rate * gradient
    users_out[...] = user_rows
    user_bf = user_rows.astype(jnp.bfloat16)
    predicted = lax.dot_general(user_bf, item_bf, nt, preferred_element_type=jnp.float32)
    misfit = jnp.where(observed, jnp.clip(rates - predicted, -CLIP_LIMIT, CLIP_LIMIT), 0.0).astype(jnp.bfloat16)
    tn = (((0,), (0,)), ((), ()))
    gradient = lax.dot_general(misfit, user_bf, tn, preferred_element_type=jnp.float32)
    items_out[...] = (1.0 - DECAY) * item_rows + item_rate * gradient


def mask_blocks(tile_rates, tile_flags):
    row_blocks, col_blocks = tile_flags.shape
    block_rows = tile_rates.shape[0] // row_blocks
    block_cols = tile_rates.shape[1] // col_blocks
    blocks = tile_rates.reshape(row_blocks, block_rows, col_blocks, block_cols)
    kept = jnp.where(tile_flags[:, None, :, None] > 0, blocks, jnp.zeros_like(blocks))
    return kept.reshape(tile_rates.shape)


def update_tile(user_rows, item_rows, tile_rates, tile_flags, user_rate, item_rate):
    rows, k = user_rows.shape
    cols = item_rows.shape[0]
    rates = mask_blocks(tile_rates, tile_flags)
    flops = 8 * rows * cols * k
    nbytes = 2 * (rows * k * 4 + cols * k * 4) + rows * cols * 2
    vmem = pl.BlockSpec(memory_space=pltpu.VMEM)
    return pl.pallas_call(
        functools.partial(tile_kernel, user_rate, item_rate),
        out_shape=(
            jax.ShapeDtypeStruct(user_rows.shape, jnp.float32),
            jax.ShapeDtypeStruct(item_rows.shape, jnp.float32),
        ),
        in_specs=[vmem, pl.BlockSpec(memory_space=pl.ANY), vmem],
        out_specs=(vmem, vmem),
        scratch_shapes=[pltpu.VMEM(item_rows.shape, jnp.float32), pltpu.SemaphoreType.DMA],
        cost_estimate=pl.CostEstimate(flops=flops, bytes_accessed=nbytes, transcendentals=0),
        compiler_params=pltpu.CompilerParams(vmem_limit_bytes=64 * 1024 * 1024),
    )(user_rows, item_rows, rates)


def body(user_factors, item_factors, ratings, block_mask):
    row_count = user_factors.shape[0]
    item_count = item_factors.shape[0]
    strata = ratings.shape[1]
    user_rate = RATE / item_count
    item_rate = RATE / row_count
    n_blk = lax.axis_size("blk")
    n_hop = lax.axis_size("hop")
    user_rows = user_factors
    item_rows = item_factors
    for stratum in range(strata):
        rates_src, flags_src = ratings, block_mask
        if stratum > 0:
            rates_src, user_rows = lax.optimization_barrier((ratings, user_rows))
        tile_rates = rates_src[:, stratum, :]
        tile_flags = flags_src[:, stratum, :]
        user_rows, item_rows = update_tile(user_rows, item_rows, tile_rates, tile_flags, user_rate, item_rate)
        if stratum < strata - 2:
            item_rows = shift(item_rows, "blk", (n_blk,), (1,))
        elif stratum == strata - 2:
            item_rows = shift(item_rows, "hop", (n_hop,), (1,))
    back = strata - 2
    returned = shift(item_rows, ("blk", "hop"), (n_blk, n_hop), (-back, -1))
    return (user_rows, returned)


def solution(mesh):
    in_specs = (
        P(("blk", "hop"), None),
        P(("blk", "hop"), None),
        P(("blk", "hop"), None, None),
        P(("blk", "hop"), None, None),
    )
    out_specs = (P(("blk", "hop"), None), P(("blk", "hop"), None))
    return jax.shard_map(body, mesh=mesh, in_specs=in_specs, out_specs=out_specs, check_vma=False)
```

```python
import functools

import jax
import jax.numpy as jnp
from jax import lax
from jax.experimental import pallas as pl
from jax.experimental.pallas import tpu as pltpu
from jax.sharding import PartitionSpec as P


CLIP_LIMIT = 3.0
DECAY = 0.03
RATE = 4.0


def shift(block, axes, sizes, offsets):
    total = 1
    for size in sizes:
        total *= size
    route = []
    for src in range(total):
        coords = []
        rem = src
        for size in reversed(sizes):
            coords.append(rem % size)
            rem //= size
        coords = coords[::-1]
        dst = 0
        for c, size, off in zip(coords, sizes, offsets):
            dst = dst * size + (c + off) % size
        route.append((src, dst))
    return lax.ppermute(block, axes, route)


NT = (((1,), (1,)), ((), ()))
TN = (((0,), (0,)), ((), ()))


def misfit_of(user_bf, item_bf, rates):
    predicted = lax.dot_general(user_bf, item_bf, NT, preferred_element_type=jnp.float32)
    misfit = jnp.where(rates != 0, jnp.clip(rates - predicted, -CLIP_LIMIT, CLIP_LIMIT), 0.0)
    return misfit.astype(jnp.bfloat16)


def user_part(users_ref, items_ref, rates_ref):
    item_bf = items_ref[...].astype(jnp.bfloat16)
    user_bf = users_ref[...].astype(jnp.bfloat16)
    misfit = misfit_of(user_bf, item_bf, rates_ref[...].astype(jnp.float32))
    return jnp.dot(misfit, item_bf, preferred_element_type=jnp.float32)


def item_part(item_rate, user_bf, items_ref, rates_ref):
    item_rows = items_ref[...]
    misfit = misfit_of(user_bf, item_rows.astype(jnp.bfloat16), rates_ref[...].astype(jnp.float32))
    gradient = lax.dot_general(misfit, user_bf, TN, preferred_element_type=jnp.float32)
    return (1.0 - DECAY) * item_rows + item_rate * gradient


def first_kernel(users_ref, items_ref, rates_ref, partial_out):
    partial_out[...] = user_part(users_ref, items_ref, rates_ref)


def middle_kernel(user_rate, item_rate, users_ref, partial_ref, items1_ref, rates1_ref, items0_ref, rates0_ref,
                  users_out, items0_out):
    gradient = partial_ref[...] + user_part(users_ref, items1_ref, rates1_ref)
    user_rows = (1.0 - DECAY) * users_ref[...] + user_rate * gradient
    users_out[...] = user_rows
    items0_out[...] = item_part(item_rate, user_rows.astype(jnp.bfloat16), items0_ref, rates0_ref)


def last_kernel(item_rate, users_ref, items_ref, rates_ref, items_out):
    items_out[...] = item_part(item_rate, users_ref[...].astype(jnp.bfloat16), items_ref, rates_ref)


def call(kernel, outs, args, flops):
    vmem = pl.BlockSpec(memory_space=pltpu.VMEM)
    nbytes = sum(a.size * a.dtype.itemsize for a in args) + sum(o.size * o.dtype.itemsize for o in outs)
    return pl.pallas_call(
        kernel,
        out_shape=tuple(outs),
        in_specs=[vmem] * len(args),
        out_specs=tuple([vmem] * len(outs)),
        cost_estimate=pl.CostEstimate(flops=flops, bytes_accessed=nbytes, transcendentals=0),
    )(*args)


def mask_blocks(tile_rates, tile_flags):
    row_blocks, col_blocks = tile_flags.shape
    block_rows = tile_rates.shape[0] // row_blocks
    block_cols = tile_rates.shape[1] // col_blocks
    blocks = tile_rates.reshape(row_blocks, block_rows, col_blocks, block_cols)
    kept = jnp.where(tile_flags[:, None, :, None] > 0, blocks, jnp.zeros_like(blocks))
    return kept.reshape(tile_rates.shape)


def body(user_factors, item_factors, ratings, block_mask):
    row_count, k = user_factors.shape
    item_count = item_factors.shape[0]
    strata = ratings.shape[1]
    user_rate = RATE / item_count
    item_rate = RATE / row_count
    n_blk = lax.axis_size("blk")
    n_hop = lax.axis_size("hop")
    half = item_count // 2
    user_rows = user_factors
    chunks = [item_factors[:half], item_factors[half:]]
    users_t = jax.ShapeDtypeStruct(user_factors.shape, jnp.float32)
    chunk_t = jax.ShapeDtypeStruct((half, k), jnp.float32)
    unit = 2 * row_count * half * k
    for stratum in range(strata):
      rates_src = ratings
      if stratum > 0:
          rates_src, user_rows = lax.optimization_barrier((ratings, user_rows))
      rates = mask_blocks(rates_src[:, stratum, :], block_mask[:, stratum, :])
      rates0, rates1 = rates[:, :half], rates[:, half:]
      (partial,) = call(first_kernel, [users_t], [user_rows, chunks[0], rates0], 2 * unit)
      user_rows, new0 = call(
          functools.partial(middle_kernel, user_rate, item_rate),
          [users_t, chunk_t],
          [user_rows, partial, chunks[1], rates1, chunks[0], rates0],
          4 * unit,
      )
      if stratum < strata - 2:
          move = functools.partial(shift, axes="blk", sizes=(n_blk,), offsets=(1,))
      elif stratum == strata - 2:
          move = functools.partial(shift, axes="hop", sizes=(n_hop,), offsets=(1,))
      else:
          move = functools.partial(shift, axes=("blk", "hop"), sizes=(n_blk, n_hop), offsets=(-(strata - 2), -1))
      new0 = move(new0)
      (new1,) = call(functools.partial(last_kernel, item_rate), [chunk_t], [user_rows, chunks[1], rates1], 2 * unit)
      new1 = move(new1)
      chunks = [new0, new1]
    return (user_rows, jnp.concatenate(chunks, axis=0))


def solution(mesh):
    in_specs = (
        P(("blk", "hop"), None),
        P(("blk", "hop"), None),
        P(("blk", "hop"), None, None),
        P(("blk", "hop"), None, None),
    )
    out_specs = (P(("blk", "hop"), None), P(("blk", "hop"), None))
    return jax.shard_map(body, mesh=mesh, in_specs=in_specs, out_specs=out_specs, check_vma=False)
```

```python
import functools

import jax
import jax.numpy as jnp
from jax import lax
from jax.experimental import pallas as pl
from jax.experimental.pallas import tpu as pltpu
from jax.sharding import PartitionSpec as P

CLIP_LIMIT = 3.0
DECAY = 0.03
RATE = 4.0


def shift(block, axes, sizes, offsets):
    total = 1
    for size in sizes:
        total *= size
    route = []
    for src in range(total):
        coords = []
        rem = src
        for size in reversed(sizes):
            coords.append(rem % size)
            rem //= size
        coords = coords[::-1]
        dst = 0
        for c, size, off in zip(coords, sizes, offsets):
            dst = dst * size + (c + off) % size
        route.append((src, dst))
    return lax.ppermute(block, axes, route)


def tile_kernel(user_rate, item_rate, users_hbm, items_hbm, rates_hbm, users_out, items_out,
                users_ref, items_ref, rates_ref, users_new, items_new, sems):
    load_users = pltpu.make_async_copy(users_hbm, users_ref, sems.at[0])
    load_items = pltpu.make_async_copy(items_hbm, items_ref, sems.at[1])
    load_rates = pltpu.make_async_copy(rates_hbm, rates_ref, sems.at[2])
    load_users.start()
    load_items.start()
    load_rates.start()
    load_items.wait()
    load_users.wait()
    user_rows = users_ref[...]
    item_rows = items_ref[...]
    item_bf = item_rows.astype(jnp.bfloat16)
    user_bf = user_rows.astype(jnp.bfloat16)
    nt = (((1,), (1,)), ((), ()))
    predicted = lax.dot_general(user_bf, item_bf, nt, preferred_element_type=jnp.float32)
    load_rates.wait()
    rates = rates_ref[...].astype(jnp.float32)
    observed = rates != 0
    misfit = jnp.where(observed, jnp.clip(rates - predicted, -CLIP_LIMIT, CLIP_LIMIT), 0.0).astype(jnp.bfloat16)
    gradient = jnp.dot(misfit, item_bf, preferred_element_type=jnp.float32)
    user_rows = (1.0 - DECAY) * user_rows + user_rate * gradient
    users_new[...] = user_rows
    store_users = pltpu.make_async_copy(users_new, users_out, sems.at[3])
    store_users.start()
    user_bf = user_rows.astype(jnp.bfloat16)
    predicted = lax.dot_general(user_bf, item_bf, nt, preferred_element_type=jnp.float32)
    misfit = jnp.where(observed, jnp.clip(rates - predicted, -CLIP_LIMIT, CLIP_LIMIT), 0.0).astype(jnp.bfloat16)
    tn = (((0,), (0,)), ((), ()))
    gradient = lax.dot_general(misfit, user_bf, tn, preferred_element_type=jnp.float32)
    items_new[...] = (1.0 - DECAY) * item_rows + item_rate * gradient
    store_items = pltpu.make_async_copy(items_new, items_out, sems.at[4])
    store_items.start()
    store_users.wait()
    store_items.wait()


def mask_blocks(tile_rates, tile_flags):
    row_blocks, col_blocks = tile_flags.shape
    block_rows = tile_rates.shape[0] // row_blocks
    block_cols = tile_rates.shape[1] // col_blocks
    blocks = tile_rates.reshape(row_blocks, block_rows, col_blocks, block_cols)
    kept = jnp.where(tile_flags[:, None, :, None] > 0, blocks, jnp.zeros_like(blocks))
    return kept.reshape(tile_rates.shape)


def update_tile(user_rows, item_rows, tile_rates, tile_flags, user_rate, item_rate):
    rows, k = user_rows.shape
    cols = item_rows.shape[0]
    rates = mask_blocks(tile_rates, tile_flags)
    flops = 8 * rows * cols * k
    nbytes = 2 * (rows * k * 4 + cols * k * 4) + rows * cols * 2
    anywhere = pl.BlockSpec(memory_space=pl.ANY)
    return pl.pallas_call(
        functools.partial(tile_kernel, user_rate, item_rate),
        out_shape=(
            jax.ShapeDtypeStruct(user_rows.shape, jnp.float32),
            jax.ShapeDtypeStruct(item_rows.shape, jnp.float32),
        ),
        in_specs=[anywhere, anywhere, anywhere],
        out_specs=(anywhere, anywhere),
        scratch_shapes=[
            pltpu.VMEM(user_rows.shape, jnp.float32),
            pltpu.VMEM(item_rows.shape, jnp.float32),
            pltpu.VMEM(rates.shape, rates.dtype),
            pltpu.VMEM(user_rows.shape, jnp.float32),
            pltpu.VMEM(item_rows.shape, jnp.float32),
            pltpu.SemaphoreType.DMA((5,)),
        ],
        cost_estimate=pl.CostEstimate(flops=flops, bytes_accessed=nbytes, transcendentals=0),
        compiler_params=pltpu.CompilerParams(),
    )(user_rows, item_rows, rates)


def body(user_factors, item_factors, ratings, block_mask):
    row_count = user_factors.shape[0]
    item_count = item_factors.shape[0]
    strata = ratings.shape[1]
    user_rate = RATE / item_count
    item_rate = RATE / row_count
    n_blk = lax.axis_size("blk")
    n_hop = lax.axis_size("hop")
    user_rows = user_factors
    item_rows = item_factors
    for stratum in range(strata):
        rates_src, flags_src = ratings, block_mask
        if stratum > 0:
            rates_src, user_rows = lax.optimization_barrier((ratings, user_rows))
        tile_rates = rates_src[:, stratum, :]
        tile_flags = flags_src[:, stratum, :]
        user_rows, item_rows = update_tile(user_rows, item_rows, tile_rates, tile_flags, user_rate, item_rate)
        if stratum < strata - 2:
            item_rows = shift(item_rows, "blk", (n_blk,), (1,))
        elif stratum == strata - 2:
            item_rows = shift(item_rows, "hop", (n_hop,), (1,))
    back = strata - 2
    returned = shift(item_rows, ("blk", "hop"), (n_blk, n_hop), (-back, -1))
    return (user_rows, returned)


def solution(mesh):
    in_specs = (
        P(("blk", "hop"), None),
        P(("blk", "hop"), None),
        P(("blk", "hop"), None, None),
        P(("blk", "hop"), None, None),
    )
    out_specs = (P(("blk", "hop"), None), P(("blk", "hop"), None))
    return jax.shard_map(body, mesh=mesh, in_specs=in_specs, out_specs=out_specs, check_vma=False)
```

```python
import functools

import jax
import jax.numpy as jnp
from jax import lax
from jax.experimental import pallas as pl
from jax.experimental.pallas import tpu as pltpu
from jax.sharding import PartitionSpec as P


CLIP_LIMIT = 3.0
DECAY = 0.03
RATE = 4.0


def shift(block, axes, sizes, offsets):
    total = 1
    for size in sizes:
        total *= size
    route = []
    for src in range(total):
        coords = []
        rem = src
        for size in reversed(sizes):
            coords.append(rem % size)
            rem //= size
        coords = coords[::-1]
        dst = 0
        for c, size, off in zip(coords, sizes, offsets):
            dst = dst * size + (c + off) % size
        route.append((src, dst))
    return lax.ppermute(block, axes, route)


def tile_kernel(user_rate, item_rate, users_ref, items_ref, rates_ref, users_out, items_out):
    rates = rates_ref[...].astype(jnp.float32)
    observed = rates != 0
    user_rows = users_ref[...]
    item_rows = items_ref[...]
    item_bf = item_rows.astype(jnp.bfloat16)
    user_bf = user_rows.astype(jnp.bfloat16)
    nt = (((1,), (1,)), ((), ()))
    predicted = lax.dot_general(user_bf, item_bf, nt, preferred_element_type=jnp.float32)
    misfit = jnp.where(observed, jnp.clip(rates - predicted, -CLIP_LIMIT, CLIP_LIMIT), 0.0).astype(jnp.bfloat16)
    gradient = jnp.dot(misfit, item_bf, preferred_element_type=jnp.float32)
    user_rows = (1.0 - DECAY) * user_rows + user_rate * gradient
    users_out[...] = user_rows
    user_bf = user_rows.astype(jnp.bfloat16)
    predicted = lax.dot_general(user_bf, item_bf, nt, preferred_element_type=jnp.float32)
    misfit = jnp.where(observed, jnp.clip(rates - predicted, -CLIP_LIMIT, CLIP_LIMIT), 0.0).astype(jnp.bfloat16)
    tn = (((0,), (0,)), ((), ()))
    gradient = lax.dot_general(misfit, user_bf, tn, preferred_element_type=jnp.float32)
    items_out[...] = (1.0 - DECAY) * item_rows + item_rate * gradient


def mask_blocks(tile_rates, tile_flags):
    row_blocks, col_blocks = tile_flags.shape
    block_rows = tile_rates.shape[0] // row_blocks
    block_cols = tile_rates.shape[1] // col_blocks
    blocks = tile_rates.reshape(row_blocks, block_rows, col_blocks, block_cols)
    kept = jnp.where(tile_flags[:, None, :, None] > 0, blocks, jnp.zeros_like(blocks))
    return kept.reshape(tile_rates.shape)


def update_tile(user_rows, item_rows, tile_rates, tile_flags, user_rate, item_rate, fuse_rates=False):
    rows, k = user_rows.shape
    cols = item_rows.shape[0]
    rates = mask_blocks(tile_rates, tile_flags)
    flops = 8 * rows * cols * k
    nbytes = 2 * (rows * k * 4 + cols * k * 4) + rows * cols * 2
    vmem = pl.BlockSpec(memory_space=pltpu.VMEM)
    return pl.pallas_call(
        functools.partial(tile_kernel, user_rate, item_rate),
        out_shape=(
            jax.ShapeDtypeStruct(user_rows.shape, jnp.float32),
            jax.ShapeDtypeStruct(item_rows.shape, jnp.float32),
        ),
        in_specs=[vmem, vmem, vmem],
        out_specs=(vmem, vmem),
        cost_estimate=pl.CostEstimate(flops=flops, bytes_accessed=nbytes, transcendentals=0),
        compiler_params=pltpu.CompilerParams(
            allow_input_fusion=[False, False, fuse_rates]
        ),
    )(user_rows, item_rows, rates)


def body(user_factors, item_factors, ratings, block_mask):
    row_count = user_factors.shape[0]
    item_count = item_factors.shape[0]
    strata = ratings.shape[1]
    user_rate = RATE / item_count
    item_rate = RATE / row_count
    n_blk = lax.axis_size("blk")
    n_hop = lax.axis_size("hop")
    user_rows = user_factors
    item_rows = item_factors
    for stratum in range(strata):
        rates_src, flags_src = ratings, block_mask
        if stratum > 0:
            rates_src, user_rows = lax.optimization_barrier((ratings, user_rows))
        tile_rates = rates_src[:, stratum, :]
        tile_flags = flags_src[:, stratum, :]
        user_rows, item_rows = update_tile(
            user_rows, item_rows, tile_rates, tile_flags, user_rate, item_rate, fuse_rates=stratum == 0
        )
        if stratum < strata - 2:
            item_rows = shift(item_rows, "blk", (n_blk,), (1,))
        elif stratum == strata - 2:
            item_rows = shift(item_rows, "hop", (n_hop,), (1,))
    back = strata - 2
    returned = shift(item_rows, ("blk", "hop"), (n_blk, n_hop), (-back, -1))
    return (user_rows, returned)


def solution(mesh):
    in_specs = (
        P(("blk", "hop"), None),
        P(("blk", "hop"), None),
        P(("blk", "hop"), None, None),
        P(("blk", "hop"), None, None),
    )
    out_specs = (P(("blk", "hop"), None), P(("blk", "hop"), None))
    return jax.shard_map(body, mesh=mesh, in_specs=in_specs, out_specs=out_specs, check_vma=False)
```

```python
import functools

import jax
import jax.numpy as jnp
from jax import lax
from jax.experimental import pallas as pl
from jax.experimental.pallas import tpu as pltpu
from jax.sharding import PartitionSpec as P


CLIP_LIMIT = 3.0
DECAY = 0.03
RATE = 4.0


def shift(block, axes, sizes, offsets):
    total = 1
    for size in sizes:
        total *= size
    route = []
    for src in range(total):
        coords = []
        rem = src
        for size in reversed(sizes):
            coords.append(rem % size)
            rem //= size
        coords = coords[::-1]
        dst = 0
        for c, size, off in zip(coords, sizes, offsets):
            dst = dst * size + (c + off) % size
        route.append((src, dst))
    return lax.ppermute(block, axes, route)


def tile_kernel(user_rate, item_rate, users_ref, items_ref, rates_ref, users_out, items_out):
    rates = rates_ref[...].astype(jnp.float32)
    observed = rates != 0
    user_rows = users_ref[...]
    item_rows = items_ref[...]
    item_bf = item_rows.astype(jnp.bfloat16)
    user_bf = user_rows.astype(jnp.bfloat16)
    nt = (((1,), (1,)), ((), ()))
    predicted = lax.dot_general(user_bf, item_bf, nt, preferred_element_type=jnp.float32)
    misfit = jnp.where(observed, jnp.clip(rates - predicted, -CLIP_LIMIT, CLIP_LIMIT), 0.0).astype(jnp.bfloat16)
    gradient = jnp.dot(misfit, item_bf, preferred_element_type=jnp.float32)
    user_rows = (1.0 - DECAY) * user_rows + user_rate * gradient
    users_out[...] = user_rows
    user_bf = user_rows.astype(jnp.bfloat16)
    predicted = lax.dot_general(user_bf, item_bf, nt, preferred_element_type=jnp.float32)
    misfit = jnp.where(observed, jnp.clip(rates - predicted, -CLIP_LIMIT, CLIP_LIMIT), 0.0).astype(jnp.bfloat16)
    tn = (((0,), (0,)), ((), ()))
    gradient = lax.dot_general(misfit, user_bf, tn, preferred_element_type=jnp.float32)
    items_out[...] = (1.0 - DECAY) * item_rows + item_rate * gradient


def mask_blocks(tile_rates, tile_flags):
    row_blocks, col_blocks = tile_flags.shape
    block_rows = tile_rates.shape[0] // row_blocks
    block_cols = tile_rates.shape[1] // col_blocks
    blocks = tile_rates.reshape(row_blocks, block_rows, col_blocks, block_cols)
    kept = jnp.where(tile_flags[:, None, :, None] > 0, blocks, jnp.zeros_like(blocks))
    return kept.reshape(tile_rates.shape)


def update_tile(user_rows, item_rows, tile_rates, tile_flags, user_rate, item_rate, fuse_rates=False):
    rows, k = user_rows.shape
    cols = item_rows.shape[0]
    rates = mask_blocks(tile_rates, tile_flags)
    flops = 8 * rows * cols * k
    nbytes = 2 * (rows * k * 4 + cols * k * 4) + rows * cols * 2
    vmem = pl.BlockSpec(memory_space=pltpu.VMEM)
    return pl.pallas_call(
        functools.partial(tile_kernel, user_rate, item_rate),
        out_shape=(
            jax.ShapeDtypeStruct(user_rows.shape, jnp.float32),
            jax.ShapeDtypeStruct(item_rows.shape, jnp.float32),
        ),
        in_specs=[vmem, vmem, vmem],
        out_specs=(vmem, vmem),
        cost_estimate=pl.CostEstimate(flops=flops, bytes_accessed=nbytes, transcendentals=0),
        compiler_params=pltpu.CompilerParams(
            allow_input_fusion=[False, False, fuse_rates]
        ),
    )(user_rows, item_rows, rates)


def body(user_factors, item_factors, ratings, block_mask):
    row_count = user_factors.shape[0]
    item_count = item_factors.shape[0]
    strata = ratings.shape[1]
    user_rate = RATE / item_count
    item_rate = RATE / row_count
    n_blk = lax.axis_size("blk")
    n_hop = lax.axis_size("hop")
    user_rows = user_factors
    item_rows = item_factors
    for stratum in range(strata):
        rates_src, flags_src = ratings, block_mask
        if stratum > 0:
            rates_src, user_rows = lax.optimization_barrier((ratings, user_rows))
        tile_rates = rates_src[:, stratum, :]
        tile_flags = flags_src[:, stratum, :]
        user_rows, item_rows = update_tile(
            user_rows, item_rows, tile_rates, tile_flags, user_rate, item_rate, fuse_rates=True
        )
        if stratum < strata - 2:
            item_rows = shift(item_rows, "blk", (n_blk,), (1,))
        elif stratum == strata - 2:
            item_rows = shift(item_rows, "hop", (n_hop,), (1,))
    back = strata - 2
    returned = shift(item_rows, ("blk", "hop"), (n_blk, n_hop), (-back, -1))
    return (user_rows, returned)


def solution(mesh):
    in_specs = (
        P(("blk", "hop"), None),
        P(("blk", "hop"), None),
        P(("blk", "hop"), None, None),
        P(("blk", "hop"), None, None),
    )
    out_specs = (P(("blk", "hop"), None), P(("blk", "hop"), None))
    return jax.shard_map(body, mesh=mesh, in_specs=in_specs, out_specs=out_specs, check_vma=False)
```
